512 devices in a mesh: mesh: 64 (over z, y), param: 8 (over x, core).
Axes of the slice: x: 4, y: 8, z: 8, core: 2. Of those that a mesh axis runs over, the one named last changes fastest.
Arguments:
- snapshots: bfloat16 [262144, 1024], P('mesh', 'param'), may hold values from -4 to 4
- coupling: bfloat16 [2048, 3, 128, 128], P('mesh'), may hold values from -0.3125 to 0.3125
- reaction_rate: float32 [1024], P('param'), may hold values from 0.1 to 1
- sketch: bfloat16 [256, 128], replicated, may hold values from -0.375 to 0.375
Outputs:
- mode_basis: bfloat16 [262144, 128], P('mesh', 'param')
The draws below stay inside these ranges and needn't reach their ends.
All inputs are finite; a program needn't handle non-finite values.
Results may differ from the reference program's by a relative error of at most 0.0095.
Values may be sent and summed in bfloat16 or wider, within the bound.
No kernel may reach another device: no remote copies, remote signals or barrier semaphores. Data moves between devices by JAX's collectives and lax.ppermute only.
A program may use at most 64 MiB of HBM per device.

```python
import math
import jax
import jax.numpy as jnp
from jax import lax

BLOCK = 128
MODES = 128
SECTIONS = 3
NBLK = 2048
ROWS = 262144
TRAJ = 1024
LEVELS = 3
N_PARAM = 8


def steps_of(rng, shape, pieces, least, top_value):
    def one(position, shards_of):
        steps = jax.random.uniform(jax.random.fold_in(jax.random.fold_in(rng, 6), position), (shards_of,), jnp.float32, least / len(pieces), top_value / len(pieces))
        return jnp.repeat(jnp.exp(steps), shape[position] // shards_of).reshape((-1,) + (1,) * (len(shape) - position - 1))

    level = one(*pieces[0])
    for cut in pieces[1:]:
        level = level * one(*cut)
    return level


def bell_draw(stream_key, shape, deviation, most, pieces=(), kind=jnp.bfloat16):
    loudness = steps_of(stream_key, shape, pieces, -0.22, 0.18) if pieces else 1.0
    result = jax.random.normal(stream_key, shape, jnp.float32) * deviation * loudness
    return jnp.minimum(jnp.maximum(result, -most), most).astype(kind)


def setup_inputs(seed: int = 0) -> dict:
    key_list = jax.random.split(jax.random.key(seed), 5)
    return {
        "snapshots": bell_draw(key_list[0], (ROWS, TRAJ), 1.0, 4.0, ((0, 64), (1, 8))),
        "coupling": bell_draw(key_list[1], (NBLK, 3, BLOCK, BLOCK), (3 * BLOCK) ** -0.5, 0.3125, ((0, 64),)),
        "reaction_rate": jnp.clip(jnp.exp(math.log(1.0) - 2.3025851 * jax.random.uniform(key_list[2], (TRAJ,), jnp.float32) ** steps_of(key_list[2], (TRAJ,), ((0, 8),), -0.2, 0.2)), 0.1, 1.0),
        "sketch": bell_draw(key_list[3], (2 * MODES, MODES), (2 * MODES) ** -0.5, 0.375),
    }


def run_sections(state, coupling, rate_row):
    block_count = state.shape[0] // BLOCK
    coupling_wide = coupling.astype(jnp.float32)
    for section_index in range(SECTIONS):
        current = state.astype(jnp.float32)
        blocks = current.reshape(block_count, BLOCK, MODES)
        zero_block = jnp.zeros((1, BLOCK, MODES), jnp.float32)
        below_blocks = jnp.concatenate([zero_block, blocks[:-1]], 0)
        above_blocks = jnp.concatenate([blocks[1:], zero_block], 0)
        stacked = jnp.stack([blocks, below_blocks, above_blocks], 1)
        mixed_rows = jnp.einsum('bkij,bkjm->bim', coupling_wide, stacked).reshape(state.shape)
        state = ((0.5 * current + 0.5 * mixed_rows) / (1.0 + rate_row[None, :] * current * current)).astype(jnp.bfloat16)
    return state

def scaled_inverse(gram_matrix):
    cholesky_lower = jnp.linalg.cholesky(gram_matrix)
    identity_matrix = jnp.eye(gram_matrix.shape[0], dtype=gram_matrix.dtype)
    inverse = jax.scipy.linalg.solve_triangular(cholesky_lower, identity_matrix, lower=True)
    return inverse.T * jnp.diagonal(cholesky_lower)[None, :]

def leaf_basis(state):
    gram_matrix = jnp.dot(state.T.astype(jnp.float32), state.astype(jnp.float32), preferred_element_type=jnp.float32)
    leaf_factor = scaled_inverse(gram_matrix).astype(jnp.bfloat16)
    return jnp.dot(state.astype(jnp.float32), leaf_factor.astype(jnp.float32), preferred_element_type=jnp.float32).astype(jnp.bfloat16)

def merge_pair(lower_basis, upper_basis, sketch):
    joined = jnp.concatenate([lower_basis, upper_basis], 1)
    merged = jnp.dot(joined.astype(jnp.float32), sketch.astype(jnp.float32), preferred_element_type=jnp.float32)
    gram_matrix = jnp.dot(merged.T, merged, precision=lax.Precision.HIGHEST)
    factor = scaled_inverse(gram_matrix)
    return jnp.dot(merged, factor, precision=lax.Precision.HIGHEST).astype(jnp.bfloat16)

def reference(snapshots, coupling, reaction_rate, sketch):
    total_rows = snapshots.shape[0]
    group_stack = snapshots.reshape(total_rows, N_PARAM, MODES).transpose(1, 0, 2)
    rate_rows = reaction_rate.reshape(N_PARAM, MODES)

    def one_group(items):
        return leaf_basis(run_sections(items[0], coupling, items[1]))
    bases = lax.map(one_group, (group_stack, rate_rows))

    def one_pair(pair_item):
        return merge_pair(pair_item[0], pair_item[1], sketch)
    for tree_level in range(LEVELS):
        pair_stack = bases.reshape(-1, 2, total_rows, MODES)
        bases = lax.map(one_pair, pair_stack)
    return bases[0]
```

```python
import jax
import jax.numpy as jnp
from jax import lax
from jax.experimental import pallas as pl
from jax.experimental.pallas import tpu as pltpu
from jax.sharding import Mesh
from jax.sharding import PartitionSpec as P

SECTIONS = 3
BLOCK = 128
GROUP = ("mesh", "core")
PANEL = 8
F32 = jnp.float32
BF16 = jnp.bfloat16


def exchange(parts, axis):
    return lax.all_to_all(parts, axis, split_axis=0, concat_axis=0, tiled=True)


def copies_to(part, axis):
    return exchange(jnp.broadcast_to(part, (lax.axis_size(axis), *part.shape)), axis)


def three_parts(values):
    high = lax.reduce_precision(values, 8, 7)
    rest = values - high
    middle = lax.reduce_precision(rest, 8, 7)
    return jnp.stack([high, middle, rest - middle]).astype(BF16)


def dot(left, right, dims, precision=lax.Precision.HIGHEST):
    return lax.dot_general(
        left, right, (dims, ((), ())), precision=precision, preferred_element_type=F32
    )


def split_dot(left, right, dims, wide):
    if wide == "right":
        high = right.astype(BF16)
        low = (right - high.astype(F32)).astype(BF16)
        return dot(left, high, dims, None) + dot(left, low, dims, None)
    high = left.astype(BF16)
    low = (left - high.astype(F32)).astype(BF16)
    return dot(high, right, dims, None) + dot(low, right, dims, None)


def eliminate(grams):
    size = grams[0].shape[0]
    lane = lax.broadcasted_iota(jnp.int32, (1, size), 1)
    sublane = lax.broadcasted_iota(jnp.int32, (PANEL, size), 0)
    row_of = lax.broadcasted_iota(jnp.int32, (size, size), 0)
    column_of = lax.broadcasted_iota(jnp.int32, (size, size), 1)
    unit = jnp.where(row_of == column_of, 1.0, 0.0).astype(F32)
    work = [(gram, unit) for gram in grams]
    done = [[] for _ in grams]
    scales = [jnp.zeros((1, size), F32) for _ in grams]
    shape = (PANEL, size)
    for start in range(0, size, PANEL):
        following = []
        for index, (gram, inverse) in enumerate(work):
            panel, panel_inverse = gram[:PANEL], inverse[:PANEL]
            value = {
                (i, j): jnp.broadcast_to(panel[i : i + 1, start + j : start + j + 1], shape)
                for i in range(PANEL)
                for j in range(i, PANEL)
            }
            rows = [jnp.broadcast_to(panel[i : i + 1], shape) for i in range(PANEL)]
            rows_inverse = [
                jnp.broadcast_to(panel_inverse[i : i + 1], shape) for i in range(PANEL)
            ]
            ratio = []
            for i in range(PANEL):
                inverse_pivot = 1.0 / value[i, i]
                ratio.append(inverse_pivot)
                scales[index] = jnp.where(
                    lane == start + i, value[i, i][:1], scales[index]
                )
                for j in range(i + 1, PANEL):
                    step = value[i, j] * inverse_pivot
                    for k in range(j, PANEL):
                        value[j, k] = value[j, k] - step * value[i, k]
                    rows[j] = rows[j] - step * rows[i]
                    rows_inverse[j] = rows_inverse[j] - step * rows_inverse[i]
            upper = jnp.zeros(shape, F32)
            finished = jnp.zeros(shape, F32)
            scaled = jnp.zeros(shape, F32)
            for i in range(PANEL):
                upper = jnp.where(sublane == i, rows[i], upper)
                scaled = jnp.where(sublane == i, rows[i] * ratio[i], scaled)
                finished = jnp.where(sublane == i, rows_inverse[i], finished)
            done[index].append(finished)
            if start + PANEL < size:
                both = jnp.concatenate([upper, finished], 1)
                update = dot(scaled, both, ((0,), (0,)))[start + PANEL :]
                following.append(
                    (gram[PANEL:] - update[:, :size], inverse[PANEL:] - update[:, size:])
                )
        work = following
    return [jnp.concatenate(parts, 0) for parts in done], scales


def sections_kernel(
    core_ref, rate_ref, snap, other, halo_own, halo_other, coupling, state_out, gram_out,
    first, second, blocks, sems,
):
    core = core_ref[0]
    away = 1 - core
    local = pl.multiple_of(384 * away, 128)
    beyond = pl.multiple_of(2432 * core, 128)
    copies = [
        (snap.at[pl.ds(pl.multiple_of(core * 1664, 128), 2432)], first.at[core, pl.ds(local, 2432)]),
        (other.at[pl.ds(0, 2432)], first.at[away, pl.ds(local, 2432)]),
        (halo_own.at[pl.ds(0, 384)], first.at[core, pl.ds(beyond, 384)]),
        (halo_other.at[pl.ds(0, 384)], first.at[away, pl.ds(beyond, 384)]),
        (coupling.at[pl.ds(core * 14 * 384, 18 * 384)], blocks.at[pl.ds(pl.multiple_of(away * 768, 128), 18 * 384)]),
        (halo_own.at[pl.ds(384, 384)], blocks.at[pl.ds(pl.multiple_of(core * 19 * 384, 128), 384)]),
        (halo_other.at[pl.ds(384, 384)], blocks.at[pl.ds(pl.multiple_of(384 + core * 17 * 384, 128), 384)]),
    ]
    started = [
        pltpu.make_async_copy(source, target, sems.at[i])
        for i, (source, target) in enumerate(copies)
    ]
    for copy in started:
        copy.start()
    for copy in started:
        copy.wait()
    rate = rate_ref[...]

    def section(source, number, store):
        def one(block, carry):
            at = pl.multiple_of(block * 128, 128)
            around = pl.multiple_of(at - 128, 128)
            matrix = pl.multiple_of((block - 1) * 384, 128)
            operator = jnp.concatenate(
                [
                    blocks[pl.ds(pl.multiple_of(matrix + 128, 128), 128)],
                    blocks[pl.ds(matrix, 128)],
                    blocks[pl.ds(pl.multiple_of(matrix + 256, 128), 128)],
                ],
                1,
            )
            window = jnp.concatenate(
                [source[0, pl.ds(around, 384)], source[1, pl.ds(around, 384)]], 1
            )
            mixed = jnp.dot(operator, window, preferred_element_type=F32)
            current = jnp.concatenate(
                [source[0, pl.ds(at, 128)], source[1, pl.ds(at, 128)]], 1
            ).astype(F32)
            new = (0.5 * current + 0.5 * mixed) / (1.0 + rate * current * current)
            store(block, new.astype(BF16))
            return carry

        lax.fori_loop(number, 22 - number, one, 0)

    def into(target):
        def store(block, value):
            at = pl.multiple_of(block * 128, 128)
            target[0, pl.ds(at, 128)] = value[:, :128]
            target[1, pl.ds(at, 128)] = value[:, 128:]

        return store

    def finish(block, value):
        state_out[pl.ds(pl.multiple_of((block - 3) * 128, 128), 128)] = value

    section(first, 1, into(second))
    section(second, 2, into(first))
    section(first, 3, finish)
    gram = jnp.zeros((256, 256), F32)
    for part in range(4):
        piece = state_out[part * 512 : part * 512 + 512]
        gram = gram + dot(piece, piece, ((0,), (0,)), None)
    gram_out[:256] = gram[:, :128]
    gram_out[256:] = gram[:, 128:]


def leaf_and_merge_kernel(gram_ref, sketch_ref, state_ref, basis_ref):
    gram = jnp.concatenate([gram_ref[:256], gram_ref[256:]], 1)
    sketch = sketch_ref[...].astype(F32)
    (lower, upper), _ = eliminate([gram[:128, :128], gram[128:, 128:]])
    mixing = jnp.concatenate(
        [dot(lower, sketch[:128], ((0,), (0,))), dot(upper, sketch[128:], ((0,), (0,)))], 0
    )
    merged_gram = dot(mixing, dot(gram, mixing, ((1,), (0,))), ((0,), (0,)))
    (merged,), (scale,) = eliminate([merged_gram])
    factor = dot(mixing, merged, ((1,), (1,)))
    high = scale.astype(BF16)
    rest = scale - high.astype(F32)
    middle = rest.astype(BF16)
    low = (rest - middle.astype(F32)).astype(BF16)
    tail = jnp.concatenate([high, middle, low, jnp.zeros((13, 128), BF16)], 0)
    for part in range(4):
        piece = state_ref[part * 512 : part * 512 + 512]
        basis_ref[part, :512] = split_dot(piece, factor, ((1,), (0,)), "right").astype(BF16)
        basis_ref[part, 512:] = tail


PAIRS = ((0, 1), (2, 3), (0, 2), (0, 3), (1, 2), (1, 3))


def cross_kernel(bases_ref, cross_ref):
    for at, (i, j) in enumerate(PAIRS):
        cross_ref[at * 128 : at * 128 + 128] = dot(
            bases_ref[i, :512], bases_ref[j, :512], ((0,), (0,)), None
        )


def last_merges_kernel(cross_ref, sketch_ref, bases_ref, out_ref):
    sketch = sketch_ref[...].astype(F32)
    top, bottom = sketch[:128], sketch[128:]
    row_of = lax.broadcasted_iota(jnp.int32, (128, 128), 0)
    column_of = lax.broadcasted_iota(jnp.int32, (128, 128), 1)
    cross = [cross_ref[at * 128 : at * 128 + 128] for at in range(6)]
    scales = []
    for i in range(4):
        tail = bases_ref[i, 512:].astype(F32)
        scales.append(tail[0:1] + tail[1:2] + tail[2:3])

    def diagonal(scale):
        return jnp.where(row_of == column_of, jnp.broadcast_to(scale, (128, 128)), 0.0)

    def joined(first, second, between):
        gram = jnp.concatenate(
            [
                jnp.concatenate([diagonal(first), between], 1),
                jnp.concatenate([between.T, diagonal(second)], 1),
            ],
            0,
        )
        return dot(sketch, dot(gram, sketch, ((1,), (0,))), ((0,), (0,)))

    pair_grams = [joined(scales[0], scales[1], cross[0]), joined(scales[2], scales[3], cross[1])]
    (low, high), (low_scale, high_scale) = eliminate(pair_grams)
    low = dot(sketch, low, ((1,), (1,)))
    high = dot(sketch, high, ((1,), (1,)))
    between = jnp.concatenate(
        [jnp.concatenate([cross[2], cross[3]], 1), jnp.concatenate([cross[4], cross[5]], 1)], 0
    )
    between = dot(low, dot(between, high, ((1,), (0,))), ((0,), (0,)))
    (root,), _ = eliminate([joined(low_scale, high_scale, between)])
    weights = jnp.concatenate(
        [
            dot(low, dot(top, root, ((1,), (1,))), ((1,), (0,))),
            dot(high, dot(bottom, root, ((1,), (1,))), ((1,), (0,))),
        ],
        0,
    )
    bases = jnp.concatenate([bases_ref[i, :512] for i in range(4)], 1)
    out_ref[...] = split_dot(weights, bases, ((0,), (1,)), "left").astype(BF16)


def call(kernel, out_shape, **options):
    return pl.pallas_call(kernel, out_shape=out_shape, **options)


def on_device(snapshots, coupling, reaction_rate, sketch):
    core = lax.axis_index("core")
    away = 1 - core
    slabs = lax.axis_size("mesh")
    operators = coupling.reshape(-1, BLOCK)

    tail = jnp.pad(three_parts(reaction_rate), ((0, 13), (0, 0)))
    wanted = lax.dynamic_slice_in_dim(snapshots, away * 1664, 2432, 0)
    other = lax.ppermute(jnp.concatenate([wanted, tail], 0), "core", [(0, 1), (1, 0)])

    def edge(above, block):
        states = lax.dynamic_slice_in_dim(snapshots, above * 3712, 384, 0)
        return jnp.concatenate([states, lax.dynamic_slice_in_dim(operators, block * 384, 384, 0)], 0)

    same, crossed = [], []
    for slab in range(slabs - 1):
        same += [(2 * slab, 2 * slab + 2), (2 * slab + 3, 2 * slab + 1)]
        crossed += [(2 * slab + 1, 2 * slab + 2), (2 * slab + 2, 2 * slab + 1)]
    halo_own = lax.ppermute(edge(away, 1 + 29 * away), GROUP, same)
    halo_other = lax.ppermute(edge(core, 31 * core), GROUP, crossed)

    other_rate = other[2432:2435].astype(F32).sum(0)
    rates = jnp.where(
        core == 0,
        jnp.concatenate([reaction_rate, other_rate]),
        jnp.concatenate([other_rate, reaction_rate]),
    )[None]
    hbm = pl.BlockSpec(memory_space=pl.ANY)
    vmem = pl.BlockSpec(memory_space=pltpu.VMEM)
    state, gram = call(
        sections_kernel,
        (jax.ShapeDtypeStruct((2048, 256), BF16), jax.ShapeDtypeStruct((512, 128), F32)),
        in_specs=[pl.BlockSpec(memory_space=pltpu.SMEM), vmem, hbm, hbm, hbm, hbm, hbm],
        out_specs=(vmem, vmem),
        scratch_shapes=[
            pltpu.VMEM((2, 2816, 128), BF16),
            pltpu.VMEM((2, 2816, 128), BF16),
            pltpu.VMEM((7680, 128), BF16),
            pltpu.SemaphoreType.DMA((7,)),
        ],
        name="sections",
    )(core[None].astype(jnp.int32), rates, snapshots, other, halo_own, halo_other, operators)

    own = exchange(gram.reshape(128, 4, 128), GROUP).sum(0)
    gram = copies_to(own, GROUP).reshape(512, 128)
    bases = call(
        leaf_and_merge_kernel, jax.ShapeDtypeStruct((4, 528, 128), BF16), name="leaf_and_merge"
    )(gram, sketch, state)
    bases = exchange(bases, "x")
    cross = call(cross_kernel, jax.ShapeDtypeStruct((768, 128), F32), name="cross")(bases)
    own = exchange(cross.reshape(128, 6, 128), GROUP).sum(0)
    own = copies_to(own, "x").sum(0)
    cross = copies_to(own, GROUP).reshape(768, 128)
    turned = call(
        last_merges_kernel, jax.ShapeDtypeStruct((128, 512), BF16), name="last_merges"
    )(cross, sketch, bases)
    turned = exchange(turned.reshape(8, 16, 512), ("x", "core"))
    return turned.reshape(4, 2, 16, 512).transpose(1, 0, 3, 2).reshape(4096, 16)


def solution(mesh):
    fine = Mesh(mesh.devices.reshape(mesh.devices.shape[0], -1, 2), ("mesh", "x", "core"))
    param = ("x", "core")
    return jax.shard_map(
        on_device,
        mesh=fine,
        in_specs=(P("mesh", param), P("mesh", None, None, None), P(param), P()),
        out_specs=P("mesh", param),
        check_vma=False,
    )
```

```python
import jax
import jax.numpy as jnp
from jax import lax
from jax.experimental import pallas as pl
from jax.experimental.pallas import tpu as pltpu
from jax.sharding import Mesh
from jax.sharding import PartitionSpec as P

SECTIONS = 3
BLOCK = 128
GROUP = ("mesh", "core")
PANEL = 16
F32 = jnp.float32
BF16 = jnp.bfloat16


def exchange(parts, axis):
    return lax.all_to_all(parts, axis, split_axis=0, concat_axis=0, tiled=True)


def copies_to(part, axis):
    return exchange(jnp.broadcast_to(part, (lax.axis_size(axis), *part.shape)), axis)


def three_parts(values):
    high = lax.reduce_precision(values, 8, 7)
    rest = values - high
    middle = lax.reduce_precision(rest, 8, 7)
    return jnp.stack([high, middle, rest - middle]).astype(BF16)


def dot(left, right, dims):
    return lax.dot_general(left, right, (dims, ((), ())), preferred_element_type=F32)


def terms_of(values, most):
    if values.dtype == BF16:
        return [values]
    terms = []
    for _ in range(most):
        terms.append(values.astype(BF16))
        values = values - terms[-1].astype(F32)
    return terms


def precise(left, right, dims, most=3):
    lefts, rights = terms_of(left, most), terms_of(right, most)
    pairs = [(i, j) for i in range(len(lefts)) for j in range(len(rights)) if i + j < most]
    return dot(
        jnp.concatenate([lefts[i] for i, _ in pairs], dims[0][0]),
        jnp.concatenate([rights[j] for _, j in pairs], dims[1][0]),
        dims,
    )


def stacked_rows(rows):
    sublane = lax.broadcasted_iota(jnp.int32, rows[0].shape, 0)
    eights = []
    for first in range(0, len(rows), 8):
        eight = rows[first]
        for i in range(1, 8):
            eight = jnp.where(sublane == i, rows[first + i], eight)
        eights.append(eight)
    return jnp.concatenate(eights, 0)


def eliminate(grams):
    size = grams[0].shape[0]
    shape = (8, size)
    lane = lax.broadcasted_iota(jnp.int32, (1, size), 1)
    row_of = lax.broadcasted_iota(jnp.int32, (size, size), 0)
    column_of = lax.broadcasted_iota(jnp.int32, (size, size), 1)
    unit = jnp.where(row_of == column_of, 1.0, 0.0).astype(F32)
    work = [(gram, unit) for gram in grams]
    done = [[] for _ in grams]
    scales = [jnp.zeros((1, size), F32) for _ in grams]
    for start in range(0, size, PANEL):
        following = []
        for index, (gram, inverse) in enumerate(work):
            value = {
                (i, j): jnp.broadcast_to(gram[i : i + 1, start + j : start + j + 1], shape)
                for i in range(PANEL)
                for j in range(i, PANEL)
            }
            rows = [jnp.broadcast_to(gram[i : i + 1], shape) for i in range(PANEL)]
            rows_inverse = [jnp.broadcast_to(inverse[i : i + 1], shape) for i in range(PANEL)]
            ratio = []
            for i in range(PANEL):
                inverse_pivot = 1.0 / value[i, i]
                ratio.append(inverse_pivot)
                scales[index] = jnp.where(lane == start + i, value[i, i][:1], scales[index])
                for j in range(i + 1, PANEL):
                    step = value[i, j] * inverse_pivot
                    for k in range(j, PANEL):
                        value[j, k] = value[j, k] - step * value[i, k]
                    rows[j] = rows[j] - step * rows[i]
                    rows_inverse[j] = rows_inverse[j] - step * rows_inverse[i]
            finished = stacked_rows(rows_inverse)
            done[index].append(finished)
            if start + PANEL < size:
                scaled = stacked_rows([row * by for row, by in zip(rows, ratio)])
                both = jnp.concatenate([stacked_rows(rows), finished], 1)
                update = precise(scaled, both, ((0,), (0,)))[start + PANEL :]
                following.append(
                    (gram[PANEL:] - update[:, :size], inverse[PANEL:] - update[:, size:])
                )
        work = following
    return [jnp.concatenate(parts, 0) for parts in done], scales


def sections_kernel(
    core_ref, rate_ref, snap, other, halo_own, halo_other, coupling, state_out, gram_out,
    first, second, blocks, sems,
):
    core = core_ref[0]
    away = 1 - core
    local = pl.multiple_of(384 * away, 128)
    beyond = pl.multiple_of(2432 * core, 128)
    copies = [
        (snap.at[pl.ds(pl.multiple_of(core * 1664, 128), 2432)], first.at[core, pl.ds(local, 2432)]),
        (other.at[pl.ds(0, 2432)], first.at[away, pl.ds(local, 2432)]),
        (halo_own.at[pl.ds(0, 384)], first.at[core, pl.ds(beyond, 384)]),
        (halo_other.at[pl.ds(0, 384)], first.at[away, pl.ds(beyond, 384)]),
        (coupling.at[pl.ds(core * 14 * 384, 18 * 384)], blocks.at[pl.ds(pl.multiple_of(away * 768, 128), 18 * 384)]),
        (halo_own.at[pl.ds(384, 384)], blocks.at[pl.ds(pl.multiple_of(core * 19 * 384, 128), 384)]),
        (halo_other.at[pl.ds(384, 384)], blocks.at[pl.ds(pl.multiple_of(384 + core * 17 * 384, 128), 384)]),
    ]
    started = [
        pltpu.make_async_copy(source, target, sems.at[i])
        for i, (source, target) in enumerate(copies)
    ]
    for copy in started:
        copy.start()
    for copy in started:
        copy.wait()
    rate = rate_ref[...]

    def section(source, number, store):
        def one(block, carry):
            at = pl.multiple_of(block * 128, 128)
            around = pl.multiple_of(at - 128, 128)
            matrix = pl.multiple_of((block - 1) * 384, 128)
            operator = jnp.concatenate(
                [
                    blocks[pl.ds(pl.multiple_of(matrix + 128, 128), 128)],
                    blocks[pl.ds(matrix, 128)],
                    blocks[pl.ds(pl.multiple_of(matrix + 256, 128), 128)],
                ],
                1,
            )
            window = jnp.concatenate(
                [source[0, pl.ds(around, 384)], source[1, pl.ds(around, 384)]], 1
            )
            mixed = jnp.dot(operator, window, preferred_element_type=F32)
            current = jnp.concatenate(
                [source[0, pl.ds(at, 128)], source[1, pl.ds(at, 128)]], 1
            ).astype(F32)
            new = (0.5 * current + 0.5 * mixed) / (1.0 + rate * current * current)
            store(block, new.astype(BF16))
            return carry

        lax.fori_loop(number, 22 - number, one, 0, unroll=True)

    def into(target):
        def store(block, value):
            at = pl.multiple_of(block * 128, 128)
            target[0, pl.ds(at, 128)] = value[:, :128]
            target[1, pl.ds(at, 128)] = value[:, 128:]

        return store

    def finish(block, value):
        state_out[pl.ds(pl.multiple_of((block - 3) * 128, 128), 128)] = value

    section(first, 1, into(second))
    section(second, 2, into(first))
    section(first, 3, finish)
    gram = jnp.zeros((256, 256), F32)
    for part in range(4):
        piece = state_out[part * 512 : part * 512 + 512]
        gram = gram + dot(piece, piece, ((0,), (0,)))
    gram_out[:256] = gram[:, :128]
    gram_out[256:] = gram[:, 128:]


def leaf_and_merge_kernel(gram_ref, sketch_ref, state_ref, basis_ref):
    gram = jnp.concatenate([gram_ref[:256], gram_ref[256:]], 1)
    sketch = sketch_ref[...]
    (lower, upper), _ = eliminate([gram[:128, :128], gram[128:, 128:]])
    mixing = jnp.concatenate(
        [precise(lower, sketch[:128], ((0,), (0,))), precise(upper, sketch[128:], ((0,), (0,)))], 0
    )
    merged_gram = precise(mixing, precise(gram, mixing, ((1,), (0,))), ((0,), (0,)))
    (merged,), (scale,) = eliminate([merged_gram])
    factor = jnp.concatenate(terms_of(precise(mixing, merged, ((1,), (1,)), 2), 2), 1)
    tail = jnp.concatenate([*terms_of(scale, 3), jnp.zeros((13, 128), BF16)], 0)
    for part in range(4):
        pieces = dot(state_ref[part * 512 : part * 512 + 512], factor, ((1,), (0,)))
        basis_ref[part, :512] = (pieces[:, :128] + pieces[:, 128:]).astype(BF16)
        basis_ref[part, 512:] = tail


PAIRS = ((0, 1), (2, 3), (0, 2), (0, 3), (1, 2), (1, 3))


def cross_kernel(bases_ref, cross_ref):
    for at, (i, j) in enumerate(PAIRS):
        cross_ref[at * 128 : at * 128 + 128] = dot(
            bases_ref[i, :512], bases_ref[j, :512], ((0,), (0,))
        )
    cross_ref[768:] = jnp.zeros((256, 128), F32)


def last_merges_kernel(cross_ref, sketch_ref, bases_ref, out_ref):
    sketch = sketch_ref[...]
    row_of = lax.broadcasted_iota(jnp.int32, (128, 128), 0)
    column_of = lax.broadcasted_iota(jnp.int32, (128, 128), 1)
    cross = [cross_ref[at * 128 : at * 128 + 128] for at in range(6)]
    scales = []
    for i in range(4):
        tail = bases_ref[i, 512:].astype(F32)
        scales.append(tail[0:1] + tail[1:2] + tail[2:3])

    def diagonal(scale):
        return jnp.where(row_of == column_of, jnp.broadcast_to(scale, (128, 128)), 0.0)

    def joined(first, second, between):
        gram = jnp.concatenate(
            [
                jnp.concatenate([diagonal(first), between], 1),
                jnp.concatenate([between.T, diagonal(second)], 1),
            ],
            0,
        )
        return precise(sketch, precise(gram, sketch, ((1,), (0,))), ((0,), (0,)))

    pair_grams = [joined(scales[0], scales[1], cross[0]), joined(scales[2], scales[3], cross[1])]
    (low, high), (low_scale, high_scale) = eliminate(pair_grams)
    low = precise(sketch, low, ((1,), (1,)))
    high = precise(sketch, high, ((1,), (1,)))
    between = jnp.concatenate(
        [jnp.concatenate([cross[2], cross[3]], 1), jnp.concatenate([cross[4], cross[5]], 1)], 0
    )
    between = precise(low, precise(between, high, ((1,), (0,))), ((0,), (0,)))
    (root,), _ = eliminate([joined(low_scale, high_scale, between)])
    mixed = precise(sketch, root, ((1,), (1,)), 2)
    weights = jnp.concatenate(
        [
            precise(low, mixed[:128], ((1,), (0,)), 2),
            precise(high, mixed[128:], ((1,), (0,)), 2),
        ],
        0,
    )
    weights = jnp.concatenate(terms_of(weights, 2), 1)
    pieces = dot(jnp.concatenate([bases_ref[i, :512] for i in range(4)], 1), weights, ((1,), (0,)))
    out_ref[...] = (pieces[:, :128] + pieces[:, 128:]).T.astype(BF16)


def call(kernel, out_shape, **options):
    return pl.pallas_call(kernel, out_shape=out_shape, **options)


def on_device(snapshots, coupling, reaction_rate, sketch):
    core = lax.axis_index("core")
    away = 1 - core
    slabs = lax.axis_size("mesh")
    operators = coupling.reshape(-1, BLOCK)

    tail = jnp.pad(three_parts(reaction_rate), ((0, 13), (0, 0)))
    wanted = lax.dynamic_slice_in_dim(snapshots, away * 1664, 2432, 0)
    other = lax.ppermute(jnp.concatenate([wanted, tail], 0), "core", [(0, 1), (1, 0)])

    def edge(above, block):
        states = lax.dynamic_slice_in_dim(snapshots, above * 3712, 384, 0)
        return jnp.concatenate([states, lax.dynamic_slice_in_dim(operators, block * 384, 384, 0)], 0)

    same, crossed = [], []
    for slab in range(slabs - 1):
        same += [(2 * slab, 2 * slab + 2), (2 * slab + 3, 2 * slab + 1)]
        crossed += [(2 * slab + 1, 2 * slab + 2), (2 * slab + 2, 2 * slab + 1)]
    halo_own = lax.ppermute(edge(away, 1 + 29 * away), GROUP, same)
    halo_other = lax.ppermute(edge(core, 31 * core), GROUP, crossed)

    other_rate = other[2432:2435].astype(F32).sum(0)
    rates = jnp.where(
        core == 0,
        jnp.concatenate([reaction_rate, other_rate]),
        jnp.concatenate([other_rate, reaction_rate]),
    )[None]
    hbm = pl.BlockSpec(memory_space=pl.ANY)
    vmem = pl.BlockSpec(memory_space=pltpu.VMEM)
    state, gram = call(
        sections_kernel,
        (jax.ShapeDtypeStruct((2048, 256), BF16), jax.ShapeDtypeStruct((512, 128), F32)),
        in_specs=[pl.BlockSpec(memory_space=pltpu.SMEM), vmem, hbm, hbm, hbm, hbm, hbm],
        out_specs=(vmem, vmem),
        scratch_shapes=[
            pltpu.VMEM((2, 2816, 128), BF16),
            pltpu.VMEM((2, 2816, 128), BF16),
            pltpu.VMEM((7680, 128), BF16),
            pltpu.SemaphoreType.DMA((7,)),
        ],
        name="sections",
    )(core[None].astype(jnp.int32), rates, snapshots, other, halo_own, halo_other, operators)

    own = exchange(gram.reshape(128, 4, 128), GROUP).sum(0)
    gram = copies_to(own, GROUP).reshape(512, 128)
    bases = call(
        leaf_and_merge_kernel, jax.ShapeDtypeStruct((4, 528, 128), BF16), name="leaf_and_merge"
    )(gram, sketch, state)
    bases = exchange(bases, "x")
    cross = call(cross_kernel, jax.ShapeDtypeStruct((1024, 128), F32), name="cross")(bases)
    own = exchange(cross.reshape(128, 8, 128), GROUP).sum(0)
    own = copies_to(own, "x").sum(0)
    cross = copies_to(own, GROUP).reshape(1024, 128)
    turned = call(
        last_merges_kernel, jax.ShapeDtypeStruct((128, 512), BF16), name="last_merges"
    )(cross, sketch, bases)
    turned = exchange(turned.reshape(8, 16, 512), ("x", "core"))
    return turned.reshape(4, 2, 16, 512).transpose(1, 0, 3, 2).reshape(4096, 16)


def solution(mesh):
    fine = Mesh(mesh.devices.reshape(mesh.devices.shape[0], -1, 2), ("mesh", "x", "core"))
    param = ("x", "core")
    return jax.shard_map(
        on_device,
        mesh=fine,
        in_specs=(P("mesh", param), P("mesh", None, None, None), P(param), P()),
        out_specs=P("mesh", param),
        check_vma=False,
    )
```

```python
import jax
import jax.numpy as jnp
from jax import lax
from jax.experimental import pallas as pl
from jax.experimental.pallas import tpu as pltpu
from jax.sharding import Mesh
from jax.sharding import PartitionSpec as P

SECTIONS = 3
BLOCK = 128
GROUP = ("mesh", "core")
PARAM = ("x", "core")
PANEL = 16
F32 = jnp.float32
BF16 = jnp.bfloat16


def exchange(parts, axis):
    return lax.all_to_all(parts, axis, split_axis=0, concat_axis=0, tiled=True)


def copies_to(part, axis):
    return exchange(jnp.broadcast_to(part, (lax.axis_size(axis), *part.shape)), axis)


def dot(left, right, dims):
    return lax.dot_general(left, right, (dims, ((), ())), preferred_element_type=F32)


def terms_of(values, most):
    if values.dtype == BF16:
        return [values]
    terms = []
    for _ in range(most):
        terms.append(values.astype(BF16))
        values = values - terms[-1].astype(F32)
    return terms


def precise(left, right, dims, most=3):
    lefts, rights = terms_of(left, most), terms_of(right, most)
    pairs = [(i, j) for i in range(len(lefts)) for j in range(len(rights)) if i + j < most]
    return dot(
        jnp.concatenate([lefts[i] for i, _ in pairs], dims[0][0]),
        jnp.concatenate([rights[j] for _, j in pairs], dims[1][0]),
        dims,
    )


def stacked_rows(rows):
    sublane = lax.broadcasted_iota(jnp.int32, rows[0].shape, 0)
    eights = []
    for first in range(0, len(rows), 8):
        eight = rows[first]
        for i in range(1, 8):
            eight = jnp.where(sublane == i, rows[first + i], eight)
        eights.append(eight)
    return jnp.concatenate(eights, 0)


def eliminate(grams):
    size = grams[0].shape[0]
    shape = (8, size)
    lane = lax.broadcasted_iota(jnp.int32, (1, size), 1)
    row_of = lax.broadcasted_iota(jnp.int32, (size, size), 0)
    column_of = lax.broadcasted_iota(jnp.int32, (size, size), 1)
    unit = jnp.where(row_of == column_of, 1.0, 0.0).astype(F32)
    work = [(gram, unit) for gram in grams]
    done = [[] for _ in grams]
    scales = [jnp.zeros((1, size), F32) for _ in grams]
    for start in range(0, size, PANEL):
        following = []
        for index, (gram, inverse) in enumerate(work):
            value = {
                (i, j): jnp.broadcast_to(gram[i : i + 1, start + j : start + j + 1], shape)
                for i in range(PANEL)
                for j in range(i, PANEL)
            }
            rows = [jnp.broadcast_to(gram[i : i + 1], shape) for i in range(PANEL)]
            rows_inverse = [jnp.broadcast_to(inverse[i : i + 1], shape) for i in range(PANEL)]
            ratio = []
            for i in range(PANEL):
                inverse_pivot = 1.0 / value[i, i]
                ratio.append(inverse_pivot)
                scales[index] = jnp.where(lane == start + i, value[i, i][:1], scales[index])
                for j in range(i + 1, PANEL):
                    step = value[i, j] * inverse_pivot
                    for k in range(j, PANEL):
                        value[j, k] = value[j, k] - step * value[i, k]
                    rows[j] = rows[j] - step * rows[i]
                    rows_inverse[j] = rows_inverse[j] - step * rows_inverse[i]
            finished = stacked_rows(rows_inverse)
            done[index].append(finished)
            if start + PANEL < size:
                scaled = stacked_rows([row * by for row, by in zip(rows, ratio)])
                both = jnp.concatenate([stacked_rows(rows), finished], 1)
                update = precise(scaled, both, ((0,), (0,)))[start + PANEL :]
                following.append(
                    (gram[PANEL:] - update[:, :size], inverse[PANEL:] - update[:, size:])
                )
        work = following
    return [jnp.concatenate(parts, 0) for parts in done], scales


def pack_kernel(core_ref, rate_ref, snap, coupling, wanted, edge_own, edge_other, sems):
    core = core_ref[0]
    away = 1 - core
    sources = [
        (snap.at[pl.ds(pl.multiple_of(away * 3712, 128), 384)], edge_own.at[pl.ds(0, 384)]),
        (coupling.at[pl.ds(pl.multiple_of(384 + 29 * 384 * away, 128), 384)], edge_own.at[pl.ds(384, 384)]),
        (snap.at[pl.ds(pl.multiple_of(core * 3712, 128), 384)], edge_other.at[pl.ds(0, 384)]),
        (coupling.at[pl.ds(pl.multiple_of(31 * 384 * core, 128), 384)], edge_other.at[pl.ds(384, 384)]),
        (snap.at[pl.ds(pl.multiple_of(away * 1664, 128), 2432)], wanted.at[pl.ds(0, 2432)]),
    ]
    copies = [pltpu.make_async_copy(*ends, sems.at[i]) for i, ends in enumerate(sources)]
    for copy in copies:
        copy.start()
    wanted[2432:] = jnp.concatenate([*terms_of(rate_ref[...], 3), jnp.zeros((13, 128), BF16)], 0)
    for copy in copies:
        copy.wait()


CHUNKS = (0, 5, 10, 14, 18)


def sections_kernel(
    core_ref, rate_ref, snap, other, halo_own, halo_other, coupling, state_out, gram_out,
    first, second, blocks, sems,
):
    core = core_ref[0]
    away = 1 - core
    local = pl.multiple_of(384 * away, 128)
    beyond = pl.multiple_of(2432 * core, 128)
    sources = [
        (snap.at[pl.ds(pl.multiple_of(core * 1664, 128), 2432)], first.at[core, pl.ds(local, 2432)]),
        (other.at[pl.ds(0, 2432)], first.at[away, pl.ds(local, 2432)]),
        (halo_own.at[pl.ds(0, 384)], first.at[core, pl.ds(beyond, 384)]),
        (halo_other.at[pl.ds(0, 384)], first.at[away, pl.ds(beyond, 384)]),
        (halo_own.at[pl.ds(384, 384)], blocks.at[pl.ds(pl.multiple_of(core * 19 * 384, 128), 384)]),
        (halo_other.at[pl.ds(384, 384)], blocks.at[pl.ds(pl.multiple_of(384 + core * 17 * 384, 128), 384)]),
    ]
    for begin, end in zip(CHUNKS, CHUNKS[1:]):
        sources.append(
            (
                coupling.at[pl.ds(pl.multiple_of((core * 14 + begin) * 384, 128), (end - begin) * 384)],
                blocks.at[pl.ds(pl.multiple_of(away * 768 + begin * 384, 128), (end - begin) * 384)],
            )
        )
    copies = [pltpu.make_async_copy(*ends, sems.at[i]) for i, ends in enumerate(sources)]
    for copy in copies:
        copy.start()
    for copy in copies[:6]:
        copy.wait()
    own_rate = rate_ref[...]
    tail = other[2432:].astype(F32)
    other_rate = tail[0:1] + tail[1:2] + tail[2:3]
    even = jnp.full((1, 128), core, jnp.int32) == 0
    rate = jnp.concatenate(
        [jnp.where(even, own_rate, other_rate), jnp.where(even, other_rate, own_rate)], 1
    )

    def section(source, number, store):
        for block in range(number, 22 - number):
            if number == 1 and block - 1 in CHUNKS[:-1]:
                copies[6 + CHUNKS.index(block - 1)].wait()
            at = block * 128
            matrix = (block - 1) * 384
            operator = jnp.concatenate(
                [
                    blocks[matrix + 128 : matrix + 256],
                    blocks[matrix : matrix + 128],
                    blocks[matrix + 256 : matrix + 384],
                ],
                1,
            )
            window = jnp.concatenate(
                [source[0, at - 128 : at + 256], source[1, at - 128 : at + 256]], 1
            )
            mixed = jnp.dot(operator, window, preferred_element_type=F32)
            current = window[128:256].astype(F32)
            new = (0.5 * current + 0.5 * mixed) / (1.0 + rate * current * current)
            store(block, new.astype(BF16))

    def into(target):
        def store(block, value):
            target[0, block * 128 : block * 128 + 128] = value[:, :128]
            target[1, block * 128 : block * 128 + 128] = value[:, 128:]

        return store

    def finish(block, value):
        state_out[(block - 3) * 128 : (block - 2) * 128] = value

    section(first, 1, into(second))
    section(second, 2, into(first))
    section(first, 3, finish)
    gram = jnp.zeros((256, 256), F32)
    for part in range(4):
        piece = state_out[part * 512 : part * 512 + 512]
        gram = gram + dot(piece, piece, ((0,), (0,)))
    gram_out[:256] = gram[:, :128]
    gram_out[256:] = gram[:, 128:]


def leaf_and_merge_kernel(gram_ref, sketch_ref, state_ref, basis_ref):
    gram = jnp.concatenate([gram_ref[:256], gram_ref[256:]], 1)
    sketch = sketch_ref[...]
    (lower, upper), _ = eliminate([gram[:128, :128], gram[128:, 128:]])
    mixing = jnp.concatenate(
        [precise(lower, sketch[:128], ((0,), (0,))), precise(upper, sketch[128:], ((0,), (0,)))], 0
    )
    merged_gram = precise(mixing, precise(gram, mixing, ((1,), (0,))), ((0,), (0,)))
    (merged,), (scale,) = eliminate([merged_gram])
    factor = jnp.concatenate(terms_of(precise(mixing, merged, ((1,), (1,)), 2), 2), 1)
    tail = jnp.concatenate([*terms_of(scale, 3), jnp.zeros((13, 128), BF16)], 0)
    for part in range(4):
        pieces = dot(state_ref[part * 512 : part * 512 + 512], factor, ((1,), (0,)))
        basis_ref[part, :512] = (pieces[:, :128] + pieces[:, 128:]).astype(BF16)
        basis_ref[part, 512:] = tail


PAIRS = ((0, 1), (2, 3), (0, 2), (0, 3), (1, 2), (1, 3))


def cross_kernel(bases_ref, cross_ref):
    for at, (i, j) in enumerate(PAIRS):
        cross_ref[at * 128 : at * 128 + 128] = dot(
            bases_ref[i, :512], bases_ref[j, :512], ((0,), (0,))
        )


def last_merges_kernel(cross_ref, sketch_ref, bases_ref, out_ref):
    sketch = sketch_ref[...]
    row_of = lax.broadcasted_iota(jnp.int32, (128, 128), 0)
    column_of = lax.broadcasted_iota(jnp.int32, (128, 128), 1)
    cross = [cross_ref[at * 128 : at * 128 + 128] for at in range(6)]
    scales = []
    for i in range(4):
        tail = bases_ref[i, 512:].astype(F32)
        scales.append(tail[0:1] + tail[1:2] + tail[2:3])

    def diagonal(scale):
        return jnp.where(row_of == column_of, jnp.broadcast_to(scale, (128, 128)), 0.0)

    def joined(first, second, between):
        gram = jnp.concatenate(
            [
                jnp.concatenate([diagonal(first), between], 1),
                jnp.concatenate([between.T, diagonal(second)], 1),
            ],
            0,
        )
        return precise(sketch, precise(gram, sketch, ((1,), (0,))), ((0,), (0,)))

    between = jnp.concatenate(
        [jnp.concatenate([cross[2], cross[3]], 1), jnp.concatenate([cross[4], cross[5]], 1)], 0
    )
    between = precise(sketch, precise(between, sketch, ((1,), (0,))), ((0,), (0,)))
    pair_grams = [joined(scales[0], scales[1], cross[0]), joined(scales[2], scales[3], cross[1])]
    (low, high), (low_scale, high_scale) = eliminate(pair_grams)
    between = precise(low, precise(between, high, ((1,), (1,))), ((1,), (0,)))
    root_gram = joined(low_scale, high_scale, between)
    weights = jnp.concatenate(
        [
            precise(sketch, precise(low, sketch[:128], ((0,), (0,))), ((1,), (0,)), 2),
            precise(sketch, precise(high, sketch[128:], ((0,), (0,))), ((1,), (0,)), 2),
        ],
        0,
    )
    (root,), _ = eliminate([root_gram])
    weights = jnp.concatenate(terms_of(precise(weights, root, ((1,), (1,)), 2), 2), 1)
    pieces = dot(jnp.concatenate([bases_ref[i, :512] for i in range(4)], 1), weights, ((1,), (0,)))
    out_ref[...] = (pieces[:, :128] + pieces[:, 128:]).T.astype(BF16)


def on_chip(values):
    return pltpu.with_memory_space_constraint(values, pltpu.VMEM)


def call(kernel, out_shape, **options):
    return pl.pallas_call(kernel, out_shape=out_shape, **options)


def on_device(snapshots, coupling, reaction_rate, sketch):
    core = lax.axis_index("core")
    slabs = lax.axis_size("mesh")
    operators = coupling.reshape(-1, BLOCK)

    same, crossed = [], []
    for slab in range(slabs - 1):
        same += [(2 * slab, 2 * slab + 2), (2 * slab + 3, 2 * slab + 1)]
        crossed += [(2 * slab + 1, 2 * slab + 2), (2 * slab + 2, 2 * slab + 1)]
    hbm = pl.BlockSpec(memory_space=pl.ANY)
    vmem = pl.BlockSpec(memory_space=pltpu.VMEM)
    smem = pl.BlockSpec(memory_space=pltpu.SMEM)
    place = core[None].astype(jnp.int32)
    rate = reaction_rate[None]
    wanted, edge_own, edge_other = call(
        pack_kernel,
        (pltpu.VMEM((2448, 128), BF16), pltpu.VMEM((768, 128), BF16), pltpu.VMEM((768, 128), BF16)),
        in_specs=[smem, vmem, hbm, hbm],
        out_specs=(vmem, vmem, vmem),
        scratch_shapes=[pltpu.SemaphoreType.DMA((5,))],
        name="pack",
    )(place, rate, snapshots, operators)
    halo_own = lax.ppermute(edge_own, GROUP, same)
    halo_other = lax.ppermute(edge_other, GROUP, crossed)
    other = lax.ppermute(wanted, "core", [(0, 1), (1, 0)])
    state, gram = call(
        sections_kernel,
        (pltpu.VMEM((2048, 256), BF16), pltpu.VMEM((512, 128), F32)),
        in_specs=[smem, vmem, hbm, vmem, vmem, vmem, hbm],
        out_specs=(vmem, vmem),
        scratch_shapes=[
            pltpu.VMEM((2, 2816, 128), BF16),
            pltpu.VMEM((2, 2816, 128), BF16),
            pltpu.VMEM((7680, 128), BF16),
            pltpu.SemaphoreType.DMA((10,)),
        ],
        name="sections",
    )(place, rate, snapshots, on_chip(other), on_chip(halo_own), on_chip(halo_other), operators)

    own = exchange(gram.reshape(128, 4, 128), GROUP).sum(0)
    gram = copies_to(own, GROUP).reshape(512, 128)
    bases = call(
        leaf_and_merge_kernel, pltpu.VMEM((4, 528, 128), BF16), name="leaf_and_merge"
    )(on_chip(gram), sketch, on_chip(state))
    bases = on_chip(exchange(bases, "x"))
    cross = call(cross_kernel, pltpu.VMEM((768, 128), F32), name="cross")(bases)
    own = exchange(cross.reshape(8, 96, 128), PARAM).sum(0)
    own = jnp.pad(own, ((0, 32), (0, 0)))
    own = copies_to(exchange(own.reshape(64, 2, 128), "mesh").sum(0), "mesh")
    cross = copies_to(own.reshape(128, 128)[:96], PARAM).reshape(768, 128)
    turned = call(
        last_merges_kernel, pltpu.VMEM((128, 512), BF16), name="last_merges"
    )(on_chip(cross), sketch, bases)
    turned = exchange(turned.reshape(8, 16, 512), PARAM)
    return turned.reshape(4, 2, 16, 512).transpose(1, 0, 3, 2).reshape(4096, 16)


def solution(mesh):
    fine = Mesh(mesh.devices.reshape(mesh.devices.shape[0], -1, 2), ("mesh", "x", "core"))
    return jax.shard_map(
        on_device,
        mesh=fine,
        in_specs=(P("mesh", PARAM), P("mesh", None, None, None), P(PARAM), P()),
        out_specs=P("mesh", PARAM),
        check_vma=False,
    )
```

```python
import jax
import jax.numpy as jnp
from jax import lax
from jax.experimental import pallas as pl
from jax.experimental.pallas import tpu as pltpu
from jax.sharding import Mesh
from jax.sharding import PartitionSpec as P

SECTIONS = 3
BLOCK = 128
GROUP = ("mesh", "core")
PARAM = ("x", "core")
PANEL = 16
F32 = jnp.float32
BF16 = jnp.bfloat16


def exchange(parts, axis):
    return lax.all_to_all(parts, axis, split_axis=0, concat_axis=0, tiled=True)


def copies_to(part, axis):
    return exchange(jnp.broadcast_to(part, (lax.axis_size(axis), *part.shape)), axis)


def dot(left, right, dims):
    return lax.dot_general(left, right, (dims, ((), ())), preferred_element_type=F32)


def terms_of(values, most):
    if values.dtype == BF16:
        return [values]
    terms = []
    for _ in range(most):
        terms.append(values.astype(BF16))
        values = values - terms[-1].astype(F32)
    return terms


def precise(left, right, dims, most=3):
    lefts, rights = terms_of(left, most), terms_of(right, most)
    pairs = [(i, j) for i in range(len(lefts)) for j in range(len(rights)) if i + j < most]
    return dot(
        jnp.concatenate([lefts[i] for i, _ in pairs], dims[0][0]),
        jnp.concatenate([rights[j] for _, j in pairs], dims[1][0]),
        dims,
    )


def stacked_rows(rows, count):
    sublane = lax.broadcasted_iota(jnp.int32, rows[0].shape, 0)
    stacks = [[] for _ in range(count)]
    for first in range(0, len(rows), 8):
        if count == 1:
            eight = rows[first]
            for i in range(1, 8):
                eight = jnp.where(sublane == i, rows[first + i], eight)
            stacks[0].append(eight)
            continue
        fours = []
        for begin in (first, first + 4):
            four = rows[begin]
            for i in range(1, 4):
                four = jnp.where(sublane % 4 == i, rows[begin + i], four)
            fours.append(four)
        upper = sublane < 4
        stacks[0].append(jnp.where(upper, fours[0], pltpu.roll(fours[1], 4, 0)))
        stacks[1].append(jnp.where(upper, pltpu.roll(fours[0], 4, 0), fours[1]))
    return [jnp.concatenate(stack, 0) for stack in stacks]


def eliminate(grams):
    count = len(grams)
    size = grams[0].shape[0]
    shape = (8, size)
    upper = lax.broadcasted_iota(jnp.int32, shape, 0) < 4
    lane = lax.broadcasted_iota(jnp.int32, shape, 1)
    row_of = lax.broadcasted_iota(jnp.int32, (size, size), 0)
    column_of = lax.broadcasted_iota(jnp.int32, (size, size), 1)
    unit = jnp.where(row_of == column_of, 1.0, 0.0).astype(F32)

    def spread(parts):
        wide = [jnp.broadcast_to(part, shape) for part in parts]
        return wide[0] if count == 1 else jnp.where(upper, *wide)

    work = [(gram, unit) for gram in grams]
    done = [[] for _ in grams]
    scales = jnp.zeros(shape, F32)
    for start in range(0, size, PANEL):
        rows = [spread([gram[i : i + 1] for gram, _ in work]) for i in range(PANEL)]
        value = {
            (i, j): jnp.broadcast_to(rows[i][:, start + j : start + j + 1], shape)
            for i in range(PANEL)
            for j in range(i, PANEL)
        }
        rows_inverse = [spread([inverse[i : i + 1] for _, inverse in work]) for i in range(PANEL)]
        ratio = []
        for i in range(PANEL):
            inverse_pivot = 1.0 / value[i, i]
            ratio.append(inverse_pivot)
            scales = jnp.where(lane == start + i, value[i, i], scales)
            for j in range(i + 1, PANEL):
                step = value[i, j] * inverse_pivot
                for k in range(j, PANEL):
                    value[j, k] = value[j, k] - step * value[i, k]
                rows[j] = rows[j] - step * rows[i]
                rows_inverse[j] = rows_inverse[j] - step * rows_inverse[i]
        finished = stacked_rows(rows_inverse, count)
        for parts, part in zip(done, finished):
            parts.append(part)
        if start + PANEL < size:
            scaled = stacked_rows([row * by for row, by in zip(rows, ratio)], count)
            reduced = stacked_rows(rows, count)
            following = []
            for index, (gram, inverse) in enumerate(work):
                both = jnp.concatenate([reduced[index], finished[index]], 1)
                update = precise(scaled[index], both, ((0,), (0,)))[start + PANEL :]
                following.append(
                    (gram[PANEL:] - update[:, :size], inverse[PANEL:] - update[:, size:])
                )
            work = following
    return [jnp.concatenate(parts, 0) for parts in done], [
        scales[4 * index : 4 * index + 1] for index in range(count)
    ]


def pack_kernel(core_ref, rate_ref, snap, coupling, wanted, edge_own, edge_other, sems):
    core = core_ref[0]
    away = 1 - core
    sources = [
        (snap.at[pl.ds(pl.multiple_of(away * 3712, 128), 384)], edge_own.at[pl.ds(0, 384)]),
        (coupling.at[pl.ds(pl.multiple_of(384 + 29 * 384 * away, 128), 384)], edge_own.at[pl.ds(384, 384)]),
        (snap.at[pl.ds(pl.multiple_of(core * 3712, 128), 384)], edge_other.at[pl.ds(0, 384)]),
        (coupling.at[pl.ds(pl.multiple_of(31 * 384 * core, 128), 384)], edge_other.at[pl.ds(384, 384)]),
        (snap.at[pl.ds(pl.multiple_of(away * 1664, 128), 2432)], wanted.at[pl.ds(0, 2432)]),
    ]
    copies = [pltpu.make_async_copy(*ends, sems.at[i]) for i, ends in enumerate(sources)]
    for copy in copies:
        copy.start()
    wanted[2432:] = jnp.concatenate([*terms_of(rate_ref[...], 3), jnp.zeros((13, 128), BF16)], 0)
    for copy in copies:
        copy.wait()


CHUNKS = (0, 5, 10, 14, 18)


def sections_kernel(
    core_ref, rate_ref, snap, other, halo_own, halo_other, coupling, state_out, gram_out,
    first, second, blocks, sems,
):
    core = core_ref[0]
    away = 1 - core
    local = pl.multiple_of(384 * away, 128)
    beyond = pl.multiple_of(2432 * core, 128)
    sources = [
        (snap.at[pl.ds(pl.multiple_of(core * 1664, 128), 2432)], first.at[core, pl.ds(local, 2432)]),
        (other.at[pl.ds(0, 2432)], first.at[away, pl.ds(local, 2432)]),
        (halo_own.at[pl.ds(0, 384)], first.at[core, pl.ds(beyond, 384)]),
        (halo_other.at[pl.ds(0, 384)], first.at[away, pl.ds(beyond, 384)]),
        (halo_own.at[pl.ds(384, 384)], blocks.at[pl.ds(pl.multiple_of(core * 19 * 384, 128), 384)]),
        (halo_other.at[pl.ds(384, 384)], blocks.at[pl.ds(pl.multiple_of(384 + core * 17 * 384, 128), 384)]),
    ]
    for begin, end in zip(CHUNKS, CHUNKS[1:]):
        sources.append(
            (
                coupling.at[pl.ds(pl.multiple_of((core * 14 + begin) * 384, 128), (end - begin) * 384)],
                blocks.at[pl.ds(pl.multiple_of(away * 768 + begin * 384, 128), (end - begin) * 384)],
            )
        )
    copies = [pltpu.make_async_copy(*ends, sems.at[i]) for i, ends in enumerate(sources)]
    for copy in copies:
        copy.start()
    for copy in copies[:6]:
        copy.wait()
    own_rate = rate_ref[...]
    tail = other[2432:].astype(F32)
    other_rate = tail[0:1] + tail[1:2] + tail[2:3]
    even = jnp.full((1, 128), core, jnp.int32) == 0
    rate = jnp.concatenate(
        [jnp.where(even, own_rate, other_rate), jnp.where(even, other_rate, own_rate)], 1
    )

    def section(source, number, store):
        for block in range(number, 22 - number):
            if number == 1 and block - 1 in CHUNKS[:-1]:
                copies[6 + CHUNKS.index(block - 1)].wait()
            at = block * 128
            matrix = (block - 1) * 384
            operator = jnp.concatenate(
                [
                    blocks[matrix + 128 : matrix + 256],
                    blocks[matrix : matrix + 128],
                    blocks[matrix + 256 : matrix + 384],
                ],
                1,
            )
            window = jnp.concatenate(
                [source[0, at - 128 : at + 256], source[1, at - 128 : at + 256]], 1
            )
            mixed = jnp.dot(operator, window, preferred_element_type=F32)
            current = window[128:256].astype(F32)
            new = (0.5 * current + 0.5 * mixed) / (1.0 + rate * current * current)
            store(block, new.astype(BF16))

    def into(target):
        def store(block, value):
            target[0, block * 128 : block * 128 + 128] = value[:, :128]
            target[1, block * 128 : block * 128 + 128] = value[:, 128:]

        return store

    def finish(block, value):
        state_out[(block - 3) * 128 : (block - 2) * 128] = value

    section(first, 1, into(second))
    section(second, 2, into(first))
    section(first, 3, finish)
    gram = jnp.zeros((256, 256), F32)
    for part in range(4):
        piece = state_out[part * 512 : part * 512 + 512]
        gram = gram + dot(piece, piece, ((0,), (0,)))
    gram_out[:256] = gram[:, :128]
    gram_out[256:] = gram[:, 128:]


def leaf_and_merge_kernel(gram_ref, sketch_ref, state_ref, basis_ref):
    gram = jnp.concatenate([gram_ref[:256], gram_ref[256:]], 1)
    sketch = sketch_ref[...]
    (lower, upper), _ = eliminate([gram[:128, :128], gram[128:, 128:]])
    mixing = jnp.concatenate(
        [precise(lower, sketch[:128], ((0,), (0,))), precise(upper, sketch[128:], ((0,), (0,)))], 0
    )
    merged_gram = precise(mixing, precise(gram, mixing, ((1,), (0,))), ((0,), (0,)))
    (merged,), _ = eliminate([merged_gram])
    factor = jnp.concatenate(terms_of(precise(mixing, merged, ((1,), (1,)), 2), 2), 1)
    for part in range(4):
        pieces = dot(state_ref[part * 512 : part * 512 + 512], factor, ((1,), (0,)))
        basis_ref[part] = (pieces[:, :128] + pieces[:, 128:]).astype(BF16)


def merge_grams_kernel(bases_ref, sketch_ref, gram_ref):
    sketch = sketch_ref[...]
    low = jnp.concatenate([bases_ref[0], bases_ref[1]], 1)
    high = jnp.concatenate([bases_ref[2], bases_ref[3]], 1)
    grams = jnp.concatenate(
        [dot(low, low, ((0,), (0,))), dot(high, high, ((0,), (0,))), dot(low, high, ((0,), (0,)))], 0
    )
    mixed = precise(grams, sketch, ((1,), (0,)))
    mixed = precise(
        sketch, jnp.concatenate([mixed[:256], mixed[256:512], mixed[512:]], 1), ((0,), (0,))
    )
    for at in range(3):
        gram_ref[at * 128 : at * 128 + 128] = mixed[:, at * 128 : at * 128 + 128]
    gram_ref[384:] = jnp.zeros((128, 128), F32)


def last_merges_kernel(gram_ref, sketch_ref, bases_ref, out_ref):
    sketch = sketch_ref[...]
    row_of = lax.broadcasted_iota(jnp.int32, (128, 128), 0)
    column_of = lax.broadcasted_iota(jnp.int32, (128, 128), 1)

    def diagonal(scale):
        return jnp.where(row_of == column_of, jnp.broadcast_to(scale, (128, 128)), 0.0)

    def joined(first, second, between):
        gram = jnp.concatenate(
            [
                jnp.concatenate([diagonal(first), between], 1),
                jnp.concatenate([between.T, diagonal(second)], 1),
            ],
            0,
        )
        return precise(sketch, precise(gram, sketch, ((1,), (0,))), ((0,), (0,)))

    (low, high), (low_scale, high_scale) = eliminate([gram_ref[:128], gram_ref[128:256]])
    between = precise(low, precise(gram_ref[256:384], high, ((1,), (1,))), ((1,), (0,)))
    root_gram = joined(low_scale, high_scale, between)
    weights = jnp.concatenate(
        [
            precise(sketch, precise(low, sketch[:128], ((0,), (0,))), ((1,), (0,)), 2),
            precise(sketch, precise(high, sketch[128:], ((0,), (0,))), ((1,), (0,)), 2),
        ],
        0,
    )
    (root,), _ = eliminate([root_gram])
    weights = jnp.concatenate(terms_of(precise(weights, root, ((1,), (1,)), 2), 2), 1)
    pieces = dot(jnp.concatenate([bases_ref[i] for i in range(4)], 1), weights, ((1,), (0,)))
    out_ref[...] = (pieces[:, :128] + pieces[:, 128:]).T.astype(BF16)


def on_chip(values):
    return pltpu.with_memory_space_constraint(values, pltpu.VMEM)


def call(kernel, out_shape, **options):
    return pl.pallas_call(kernel, out_shape=out_shape, **options)


def on_device(snapshots, coupling, reaction_rate, sketch):
    core = lax.axis_index("core")
    slabs = lax.axis_size("mesh")
    operators = coupling.reshape(-1, BLOCK)

    same, crossed = [], []
    for slab in range(slabs - 1):
        same += [(2 * slab, 2 * slab + 2), (2 * slab + 3, 2 * slab + 1)]
        crossed += [(2 * slab + 1, 2 * slab + 2), (2 * slab + 2, 2 * slab + 1)]
    hbm = pl.BlockSpec(memory_space=pl.ANY)
    vmem = pl.BlockSpec(memory_space=pltpu.VMEM)
    smem = pl.BlockSpec(memory_space=pltpu.SMEM)
    place = core[None].astype(jnp.int32)
    rate = reaction_rate[None]
    wanted, edge_own, edge_other = call(
        pack_kernel,
        (pltpu.VMEM((2448, 128), BF16), pltpu.VMEM((768, 128), BF16), pltpu.VMEM((768, 128), BF16)),
        in_specs=[smem, vmem, hbm, hbm],
        out_specs=(vmem, vmem, vmem),
        scratch_shapes=[pltpu.SemaphoreType.DMA((5,))],
        name="pack",
    )(place, rate, snapshots, operators)
    halo_own = lax.ppermute(edge_own, GROUP, same)
    halo_other = lax.ppermute(edge_other, GROUP, crossed)
    other = lax.ppermute(wanted, "core", [(0, 1), (1, 0)])
    state, gram = call(
        sections_kernel,
        (pltpu.VMEM((2048, 256), BF16), pltpu.VMEM((512, 128), F32)),
        in_specs=[smem, vmem, hbm, vmem, vmem, vmem, hbm],
        out_specs=(vmem, vmem),
        scratch_shapes=[
            pltpu.VMEM((2, 2816, 128), BF16),
            pltpu.VMEM((2, 2816, 128), BF16),
            pltpu.VMEM((7680, 128), BF16),
            pltpu.SemaphoreType.DMA((10,)),
        ],
        name="sections",
    )(place, rate, snapshots, on_chip(other), on_chip(halo_own), on_chip(halo_other), operators)

    own = exchange(gram.reshape(128, 4, 128), GROUP).sum(0)
    gram = copies_to(own, GROUP).reshape(512, 128)
    bases = call(
        leaf_and_merge_kernel, pltpu.VMEM((4, 512, 128), BF16), name="leaf_and_merge"
    )(on_chip(gram), sketch, on_chip(state))
    bases = on_chip(exchange(bases, "x"))
    gram = call(merge_grams_kernel, pltpu.VMEM((512, 128), F32), name="merge_grams")(bases, sketch)
    own = exchange(gram.reshape(128, 4, 128), GROUP).sum(0)
    own = copies_to(own, "x").sum(0)
    gram = copies_to(own, GROUP).reshape(512, 128)
    turned = call(
        last_merges_kernel, pltpu.VMEM((128, 512), BF16), name="last_merges"
    )(on_chip(gram), sketch, bases)
    turned = exchange(turned.reshape(8, 16, 512), PARAM)
    return turned.reshape(4, 2, 16, 512).transpose(1, 0, 3, 2).reshape(4096, 16)


def solution(mesh):
    fine = Mesh(mesh.devices.reshape(mesh.devices.shape[0], -1, 2), ("mesh", "x", "core"))
    return jax.shard_map(
        on_device,
        mesh=fine,
        in_specs=(P("mesh", PARAM), P("mesh", None, None, None), P(PARAM), P()),
        out_specs=P("mesh", PARAM),
        check_vma=False,
    )
```

```python
import jax
import jax.numpy as jnp
from jax import lax
from jax.experimental import pallas as pl
from jax.experimental.pallas import tpu as pltpu
from jax.sharding import Mesh
from jax.sharding import PartitionSpec as P

SECTIONS = 3
BLOCK = 128
GROUP = ("mesh", "core")
PARAM = ("x", "core")
PANEL = 16
F32 = jnp.float32
BF16 = jnp.bfloat16


def exchange(parts, axis):
    return lax.all_to_all(parts, axis, split_axis=0, concat_axis=0, tiled=True)


def copies_to(part, axis):
    return exchange(jnp.broadcast_to(part, (lax.axis_size(axis), *part.shape)), axis)


def dot(left, right, dims):
    return lax.dot_general(left, right, (dims, ((), ())), preferred_element_type=F32)


def terms_of(values, most):
    if values.dtype == BF16:
        return [values]
    terms = []
    for _ in range(most):
        terms.append(values.astype(BF16))
        values = values - terms[-1].astype(F32)
    return terms


def precise(left, right, dims, most=3):
    lefts, rights = terms_of(left, most), terms_of(right, most)
    pairs = [(i, j) for i in range(len(lefts)) for j in range(len(rights)) if i + j < most]
    return dot(
        jnp.concatenate([lefts[i] for i, _ in pairs], dims[0][0]),
        jnp.concatenate([rights[j] for _, j in pairs], dims[1][0]),
        dims,
    )


def stacked_rows(rows, count):
    sublane = lax.broadcasted_iota(jnp.int32, rows[0].shape, 0)
    stacks = [[] for _ in range(count)]
    for first in range(0, len(rows), 8):
        if count == 1:
            eight = rows[first]
            for i in range(1, 8):
                eight = jnp.where(sublane == i, rows[first + i], eight)
            stacks[0].append(eight)
            continue
        fours = []
        for begin in (first, first + 4):
            four = rows[begin]
            for i in range(1, 4):
                four = jnp.where(sublane % 4 == i, rows[begin + i], four)
            fours.append(four)
        upper = sublane < 4
        stacks[0].append(jnp.where(upper, fours[0], pltpu.roll(fours[1], 4, 0)))
        stacks[1].append(jnp.where(upper, pltpu.roll(fours[0], 4, 0), fours[1]))
    return [jnp.concatenate(stack, 0) for stack in stacks]


def eliminate(grams):
    count = len(grams)
    size = grams[0].shape[0]
    shape = (8, size)
    upper = lax.broadcasted_iota(jnp.int32, shape, 0) < 4
    lane = lax.broadcasted_iota(jnp.int32, shape, 1)
    row_of = lax.broadcasted_iota(jnp.int32, (size, size), 0)
    column_of = lax.broadcasted_iota(jnp.int32, (size, size), 1)
    unit = jnp.where(row_of == column_of, 1.0, 0.0).astype(F32)

    def spread(parts):
        wide = [jnp.broadcast_to(part, shape) for part in parts]
        return wide[0] if count == 1 else jnp.where(upper, *wide)

    work = [(gram, unit) for gram in grams]
    done = [[] for _ in grams]
    scales = jnp.zeros(shape, F32)
    for start in range(0, size, PANEL):
        rows = [spread([gram[i : i + 1] for gram, _ in work]) for i in range(PANEL)]
        value = {
            (i, j): jnp.broadcast_to(rows[i][:, start + j : start + j + 1], shape)
            for i in range(PANEL)
            for j in range(i, PANEL)
        }
        rows_inverse = [spread([inverse[i : i + 1] for _, inverse in work]) for i in range(PANEL)]
        ratio = []
        for i in range(PANEL):
            inverse_pivot = 1.0 / value[i, i]
            ratio.append(inverse_pivot)
            scales = jnp.where(lane == start + i, value[i, i], scales)
            for j in range(i + 1, PANEL):
                step = value[i, j] * inverse_pivot
                for k in range(j, PANEL):
                    value[j, k] = value[j, k] - step * value[i, k]
                rows[j] = rows[j] - step * rows[i]
                rows_inverse[j] = rows_inverse[j] - step * rows_inverse[i]
        finished = stacked_rows(rows_inverse, count)
        for parts, part in zip(done, finished):
            parts.append(part)
        if start + PANEL < size:
            scaled = stacked_rows([row * by for row, by in zip(rows, ratio)], count)
            reduced = stacked_rows(rows, count)
            following = []
            for index, (gram, inverse) in enumerate(work):
                both = jnp.concatenate([reduced[index], finished[index]], 1)
                update = precise(scaled[index], both, ((0,), (0,)))[start + PANEL :]
                following.append(
                    (gram[PANEL:] - update[:, :size], inverse[PANEL:] - update[:, size:])
                )
            work = following
    return [jnp.concatenate(parts, 0) for parts in done], [
        scales[4 * index : 4 * index + 1] for index in range(count)
    ]


def pack_kernel(core_ref, rate_ref, snap, coupling, wanted, edge_own, edge_other, sems):
    core = core_ref[0]
    away = 1 - core
    sources = [
        (snap.at[pl.ds(pl.multiple_of(away * 3712, 128), 384)], edge_own.at[pl.ds(0, 384)]),
        (coupling.at[pl.ds(pl.multiple_of(384 + 29 * 384 * away, 128), 384)], edge_own.at[pl.ds(384, 384)]),
        (snap.at[pl.ds(pl.multiple_of(core * 3712, 128), 384)], edge_other.at[pl.ds(0, 384)]),
        (coupling.at[pl.ds(pl.multiple_of(31 * 384 * core, 128), 384)], edge_other.at[pl.ds(384, 384)]),
        (snap.at[pl.ds(pl.multiple_of(away * 1664, 128), 2432)], wanted.at[pl.ds(0, 2432)]),
    ]
    copies = [pltpu.make_async_copy(*ends, sems.at[i]) for i, ends in enumerate(sources)]
    for copy in copies:
        copy.start()
    wanted[2432:] = jnp.concatenate([*terms_of(rate_ref[...], 3), jnp.zeros((13, 128), BF16)], 0)
    for copy in copies:
        copy.wait()


CHUNKS = (0, 5, 10, 14, 18)


def sections_kernel(
    core_ref, rate_ref, snap, other, halo_own, halo_other, coupling, state_out, gram_out,
    first, second, blocks, sems,
):
    core = core_ref[0]
    away = 1 - core
    local = pl.multiple_of(384 * away, 128)
    beyond = pl.multiple_of(2432 * core, 128)
    sources = [
        (snap.at[pl.ds(pl.multiple_of(core * 1664, 128), 2432)], first.at[core, pl.ds(local, 2432)]),
        (other.at[pl.ds(0, 2432)], first.at[away, pl.ds(local, 2432)]),
        (halo_own.at[pl.ds(0, 384)], first.at[core, pl.ds(beyond, 384)]),
        (halo_other.at[pl.ds(0, 384)], first.at[away, pl.ds(beyond, 384)]),
        (halo_own.at[pl.ds(384, 384)], blocks.at[pl.ds(pl.multiple_of(core * 19 * 384, 128), 384)]),
        (halo_other.at[pl.ds(384, 384)], blocks.at[pl.ds(pl.multiple_of(384 + core * 17 * 384, 128), 384)]),
    ]
    for begin, end in zip(CHUNKS, CHUNKS[1:]):
        sources.append(
            (
                coupling.at[pl.ds(pl.multiple_of((core * 14 + begin) * 384, 128), (end - begin) * 384)],
                blocks.at[pl.ds(pl.multiple_of(away * 768 + begin * 384, 128), (end - begin) * 384)],
            )
        )
    copies = [pltpu.make_async_copy(*ends, sems.at[i]) for i, ends in enumerate(sources)]
    for copy in copies:
        copy.start()
    for copy in copies[:6]:
        copy.wait()
    own_rate = rate_ref[...]
    tail = other[2432:].astype(F32)
    other_rate = tail[0:1] + tail[1:2] + tail[2:3]
    even = jnp.full((1, 128), core, jnp.int32) == 0
    rate = jnp.concatenate(
        [jnp.where(even, own_rate, other_rate), jnp.where(even, other_rate, own_rate)], 1
    )

    def section(source, number, store):
        for block in range(number, 22 - number):
            if number == 1 and block - 1 in CHUNKS[:-1]:
                copies[6 + CHUNKS.index(block - 1)].wait()
            at = block * 128
            matrix = (block - 1) * 384
            operator = jnp.concatenate(
                [
                    blocks[matrix + 128 : matrix + 256],
                    blocks[matrix : matrix + 128],
                    blocks[matrix + 256 : matrix + 384],
                ],
                1,
            )
            window = jnp.concatenate(
                [source[0, at - 128 : at + 256], source[1, at - 128 : at + 256]], 1
            )
            mixed = jnp.dot(operator, window, preferred_element_type=F32)
            current = window[128:256].astype(F32)
            new = (0.5 * current + 0.5 * mixed) / (1.0 + rate * current * current)
            store(block, new.astype(BF16))

    def into(target):
        def store(block, value):
            target[0, block * 128 : block * 128 + 128] = value[:, :128]
            target[1, block * 128 : block * 128 + 128] = value[:, 128:]

        return store

    def finish(block, value):
        state_out[(block - 3) * 128 : (block - 2) * 128] = value

    section(first, 1, into(second))
    section(second, 2, into(first))
    section(first, 3, finish)
    gram = jnp.zeros((256, 256), F32)
    for part in range(4):
        piece = state_out[part * 512 : part * 512 + 512]
        gram = gram + dot(piece, piece, ((0,), (0,)))
    gram_out[:256] = gram[:, :128]
    gram_out[256:] = gram[128:, 128:]


def leaf_and_merge_kernel(gram_ref, sketch_ref, state_ref, basis_ref):
    across = gram_ref[128:256]
    gram = jnp.concatenate(
        [gram_ref[:256], jnp.concatenate([across.T, gram_ref[256:]], 0)], 1
    )
    sketch = sketch_ref[...]
    (lower, upper), _ = eliminate([gram[:128, :128], gram[128:, 128:]])
    mixing = jnp.concatenate(
        [precise(lower, sketch[:128], ((0,), (0,))), precise(upper, sketch[128:], ((0,), (0,)))], 0
    )
    merged_gram = precise(mixing, precise(gram, mixing, ((1,), (0,))), ((0,), (0,)))
    (merged,), _ = eliminate([merged_gram])
    factor = jnp.concatenate(terms_of(precise(mixing, merged, ((1,), (1,)), 2), 2), 1)
    for part in range(4):
        pieces = dot(state_ref[part * 512 : part * 512 + 512], factor, ((1,), (0,)))
        basis_ref[part] = (pieces[:, :128] + pieces[:, 128:]).astype(BF16)


def merge_grams_kernel(bases_ref, sketch_ref, gram_ref):
    sketch = sketch_ref[...]
    low = jnp.concatenate([bases_ref[0], bases_ref[1]], 1)
    high = jnp.concatenate([bases_ref[2], bases_ref[3]], 1)
    grams = jnp.concatenate(
        [dot(low, low, ((0,), (0,))), dot(high, high, ((0,), (0,))), dot(low, high, ((0,), (0,)))], 0
    )
    mixed = precise(grams, sketch, ((1,), (0,)))
    mixed = precise(
        sketch, jnp.concatenate([mixed[:256], mixed[256:512], mixed[512:]], 1), ((0,), (0,))
    )
    for at in range(3):
        gram_ref[at * 128 : at * 128 + 128] = mixed[:, at * 128 : at * 128 + 128]


def last_merges_kernel(gram_ref, sketch_ref, bases_ref, out_ref):
    sketch = sketch_ref[...]
    row_of = lax.broadcasted_iota(jnp.int32, (128, 128), 0)
    column_of = lax.broadcasted_iota(jnp.int32, (128, 128), 1)

    def diagonal(scale):
        return jnp.where(row_of == column_of, jnp.broadcast_to(scale, (128, 128)), 0.0)

    def joined(first, second, between):
        gram = jnp.concatenate(
            [
                jnp.concatenate([diagonal(first), between], 1),
                jnp.concatenate([between.T, diagonal(second)], 1),
            ],
            0,
        )
        return precise(sketch, precise(gram, sketch, ((1,), (0,))), ((0,), (0,)))

    (low, high), (low_scale, high_scale) = eliminate([gram_ref[:128], gram_ref[128:256]])
    between = precise(low, precise(gram_ref[256:384], high, ((1,), (1,))), ((1,), (0,)))
    root_gram = joined(low_scale, high_scale, between)
    weights = jnp.concatenate(
        [
            precise(sketch, precise(low, sketch[:128], ((0,), (0,))), ((1,), (0,)), 2),
            precise(sketch, precise(high, sketch[128:], ((0,), (0,))), ((1,), (0,)), 2),
        ],
        0,
    )
    (root,), _ = eliminate([root_gram])
    weights = jnp.concatenate(terms_of(precise(weights, root, ((1,), (1,)), 2), 2), 1)
    pieces = dot(jnp.concatenate([bases_ref[i] for i in range(4)], 1), weights, ((1,), (0,)))
    out_ref[...] = (pieces[:, :128] + pieces[:, 128:]).T.astype(BF16)


def on_chip(values):
    return pltpu.with_memory_space_constraint(values, pltpu.VMEM)


def call(kernel, out_shape, **options):
    return pl.pallas_call(kernel, out_shape=out_shape, **options)


def on_device(snapshots, coupling, reaction_rate, sketch):
    core = lax.axis_index("core")
    slabs = lax.axis_size("mesh")
    operators = coupling.reshape(-1, BLOCK)

    same, crossed = [], []
    for slab in range(slabs - 1):
        same += [(2 * slab, 2 * slab + 2), (2 * slab + 3, 2 * slab + 1)]
        crossed += [(2 * slab + 1, 2 * slab + 2), (2 * slab + 2, 2 * slab + 1)]
    hbm = pl.BlockSpec(memory_space=pl.ANY)
    vmem = pl.BlockSpec(memory_space=pltpu.VMEM)
    smem = pl.BlockSpec(memory_space=pltpu.SMEM)
    place = core[None].astype(jnp.int32)
    rate = reaction_rate[None]
    wanted, edge_own, edge_other = call(
        pack_kernel,
        (pltpu.VMEM((2448, 128), BF16), pltpu.VMEM((768, 128), BF16), pltpu.VMEM((768, 128), BF16)),
        in_specs=[smem, vmem, hbm, hbm],
        out_specs=(vmem, vmem, vmem),
        scratch_shapes=[pltpu.SemaphoreType.DMA((5,))],
        name="pack",
    )(place, rate, snapshots, operators)
    halo_own = lax.ppermute(edge_own, GROUP, same)
    halo_other = lax.ppermute(edge_other, GROUP, crossed)
    other = lax.ppermute(wanted, "core", [(0, 1), (1, 0)])
    state, gram = call(
        sections_kernel,
        (pltpu.VMEM((2048, 256), BF16), pltpu.VMEM((384, 128), F32)),
        in_specs=[smem, vmem, hbm, vmem, vmem, vmem, hbm],
        out_specs=(vmem, vmem),
        scratch_shapes=[
            pltpu.VMEM((2, 2816, 128), BF16),
            pltpu.VMEM((2, 2816, 128), BF16),
            pltpu.VMEM((7680, 128), BF16),
            pltpu.SemaphoreType.DMA((10,)),
        ],
        name="sections",
    )(place, rate, snapshots, on_chip(other), on_chip(halo_own), on_chip(halo_other), operators)

    own = exchange(gram.reshape(128, 1, 384), GROUP).sum(0)
    gram = copies_to(own, GROUP).reshape(384, 128)
    bases = call(
        leaf_and_merge_kernel, pltpu.VMEM((4, 512, 128), BF16), name="leaf_and_merge"
    )(on_chip(gram), sketch, on_chip(state))
    bases = on_chip(exchange(bases, "x"))
    gram = call(merge_grams_kernel, pltpu.VMEM((384, 128), F32), name="merge_grams")(bases, sketch)
    own = exchange(gram.reshape(128, 1, 384), GROUP).sum(0)
    own = copies_to(own, "x").sum(0)
    gram = copies_to(own, GROUP).reshape(384, 128)
    turned = call(
        last_merges_kernel, pltpu.VMEM((128, 512), BF16), name="last_merges"
    )(on_chip(gram), sketch, bases)
    turned = exchange(turned.reshape(8, 16, 512), PARAM)
    return turned.reshape(4, 2, 16, 512).transpose(1, 0, 3, 2).reshape(4096, 16)


def solution(mesh):
    fine = Mesh(mesh.devices.reshape(mesh.devices.shape[0], -1, 2), ("mesh", "x", "core"))
    return jax.shard_map(
        on_device,
        mesh=fine,
        in_specs=(P("mesh", PARAM), P("mesh", None, None, None), P(PARAM), P()),
        out_specs=P("mesh", PARAM),
        check_vma=False,
    )
```
